32 devices in a mesh: groups: 2 (over x), mp: 16 (over z, y, core).
Axes of the slice: x: 2, y: 2, z: 4, core: 2. Of those that a mesh axis runs over, the one named last changes fastest.
Arguments:
- activations: bfloat16 [128, 16384], P(('groups', 'mp')), parts along dimension 0, may hold values from -6 to 6
- gain: bfloat16 [16384], replicated, may hold values from 0.5 to 1.5
- q_weight: bfloat16 [16384, 16384], P(None, 'mp'), may hold values from -0.046875 to 0.046875
- kv_weight: bfloat16 [16384, 2048], P(None, 'mp'), may hold values from -0.046875 to 0.046875
- o_weight: bfloat16 [16384, 16384], P(None, 'mp'), may hold values from -0.75 to 0.75
- key_cache: bfloat16 [128, 8, 512, 128], P(('groups', 'mp')), parts along dimension 0, may hold values from -400 to 400
- value_cache: bfloat16 [128, 8, 512, 128], P(('groups', 'mp')), parts along dimension 0, may hold values from -6 to 6
- lengths: int32 [128], P(('groups', 'mp')), parts along dimension 0, may hold values from 1 to 512, as said below
Outputs:
- attention_out: bfloat16 [128, 16384], P('groups', 'mp'), parts along dimension 0
The draws below stay inside these ranges and needn't reach their ends.
There are 2 independent parts, one for each index of `groups`. The reference program is written for one: setup_inputs(seed, part) draws one part's arguments, and reference() takes and returns one part's arrays. A program takes and returns all parts, laid end to end along the dimension named above; an argument that names none is the same for every part. Nothing has to cross between parts.
Inputs may be any that keep to these rules, and one draw needn't show every extreme that they name: Request b attends to key_cache[b, :, t] and value_cache[b, :, t] for t < lengths[b]; some request has exactly 512.
All inputs are finite; a program needn't handle non-finite values.
Results may differ from the reference program's by a relative error of at most 0.007.
The reference program's roundings to bfloat16 on the way (of `normed` and `attended`) count: a program that leaves them out, or rounds other values in their place, can miss the bound.
Values may be sent and summed in bfloat16 or wider, within the bound.
A program may use at most 128 MiB of HBM per device.

```python
import math
import jax
import jax.numpy as jnp
from jax import lax

D = 16384
HEADS = 128
KV_HEADS = 8
HEAD_DIM = 128
CACHE = 512
BATCH = 64


def draw_key_cache(key, part):
    shape = (BATCH, KV_HEADS, CACHE, HEAD_DIM)
    base = jax.random.normal(jax.random.fold_in(key, 11), shape, jnp.float32)
    return jnp.clip(base, -400.0, 400.0).astype(jnp.bfloat16)


def draw_lengths(key, part):
    drawn = jax.random.randint(jax.random.fold_in(key, 21), (BATCH,), 1, CACHE + 1, dtype=jnp.int32)
    chosen = jax.random.randint(jax.random.fold_in(key, 22), (), 0, BATCH, dtype=jnp.int32)
    return jnp.where(jnp.arange(BATCH, dtype=jnp.int32) == chosen, CACHE, drawn).astype(jnp.int32)


def levels(rng, shape, pieces, smallest, largest):
    factor_of = 1.0
    for axis_at, shards_of in pieces:
        draws = jax.random.uniform(jax.random.fold_in(jax.random.fold_in(rng, 6), axis_at), (shards_of,), jnp.float32, smallest / len(pieces), largest / len(pieces))
        factor_of = factor_of * jnp.repeat(jnp.exp(draws), shape[axis_at] // shards_of).reshape((-1,) + (1,) * (len(shape) - 1 - axis_at))
    return factor_of


def scatter_about(key, dims, scale, reach, split=(), kind=jnp.bfloat16):
    factor_of = levels(key, dims, split, -0.22, 0.18) if split else 1.0
    result = jax.random.normal(key, dims, jnp.float32) * scale * factor_of
    return jnp.minimum(jnp.maximum(result, -reach), reach).astype(kind)


def setup_inputs(seed: int = 0, part: int = 0) -> dict:
    streams_of = jax.random.split(jax.random.key(seed), 9)
    own_keys = jax.random.split(jax.random.fold_in(streams_of[8], part), 9)
    return {
        "activations": scatter_about(own_keys[0], (BATCH, D), 1.0, 6.0, ((0, 16),)),
        "gain": jnp.clip(1.0 + 0.1 * jax.random.normal(streams_of[1], (D,), jnp.float32), 0.5, 1.5).astype(jnp.bfloat16),
        "q_weight": scatter_about(streams_of[2], (D, HEADS * HEAD_DIM), D ** -0.5, 0.046875, ((1, 16),)),
        "kv_weight": scatter_about(streams_of[3], (D, 2 * KV_HEADS * HEAD_DIM), D ** -0.5, 0.046875, ((1, 16),)),
        "o_weight": scatter_about(streams_of[4], (HEADS * HEAD_DIM, D), 0.125, 0.75, ((1, 16),)),
        "key_cache": draw_key_cache(jax.random.fold_in(jax.random.fold_in(streams_of[8], part), 71), part),
        "value_cache": scatter_about(own_keys[6], (BATCH, KV_HEADS, CACHE, HEAD_DIM), 1.0, 6.0, ((0, 16),)),
        "lengths": draw_lengths(jax.random.fold_in(jax.random.fold_in(streams_of[8], part), 71), part),
    }


rope_base = 500000.0
norm_eps = 1e-05

def rotate(vector, position):
    middle = vector.shape[-1] // 2
    offsets = jnp.arange(middle, dtype=jnp.float32)
    frequency = jnp.exp(offsets * (-2.0 * math.log(rope_base) / vector.shape[-1]))
    angles = position * frequency
    cosine = jnp.cos(angles)
    sine = jnp.sin(angles)
    leading = vector[..., :middle]
    trailing = vector[..., middle:]
    return jnp.concatenate([leading * cosine - trailing * sine, trailing * cosine + leading * sine], axis=-1)

def normalize(activations, gain):
    widened = activations.astype(jnp.float32)
    inverse = lax.rsqrt(lax.optimization_barrier(jnp.mean(widened * widened, axis=-1, keepdims=True)) + norm_eps)
    return (widened * inverse * gain.astype(jnp.float32)).astype(jnp.bfloat16)

def one_request(items):
    query_row, pair_row, key_rows, value_rows, length = items
    per_group = HEADS // KV_HEADS
    position = length.astype(jnp.float32)
    scaling = 1.0 / math.sqrt(HEAD_DIM)
    query = rotate(query_row.astype(jnp.float32).reshape(KV_HEADS, per_group, HEAD_DIM), position).astype(jnp.bfloat16)
    fresh_key = rotate(pair_row[:KV_HEADS * HEAD_DIM].astype(jnp.float32).reshape(KV_HEADS, HEAD_DIM), position).astype(jnp.bfloat16)
    fresh_value = pair_row[KV_HEADS * HEAD_DIM:].reshape(KV_HEADS, HEAD_DIM)
    scores = jnp.einsum('gqd,gtd->gqt', query.astype(jnp.float32), key_rows.astype(jnp.float32)) * scaling
    visible = jnp.arange(CACHE, dtype=jnp.int32) < length
    scores = jnp.where(visible[None, None, :], scores, -1e+30)
    own = jnp.einsum('gqd,gd->gq', query.astype(jnp.float32), fresh_key.astype(jnp.float32)) * scaling
    highest = jnp.maximum(lax.optimization_barrier(jnp.max(scores, axis=-1)), own)
    weights = jnp.where(visible[None, None, :], jnp.exp(scores - highest[..., None]), 0.0)
    own_weight = jnp.exp(own - highest)
    denominator = lax.optimization_barrier(jnp.sum(weights, axis=-1)) + own_weight
    probs = (weights / denominator[..., None]).astype(jnp.bfloat16)
    own_prob = (own_weight / denominator).astype(jnp.bfloat16)
    mixed = jnp.einsum('gqt,gtd->gqd', probs.astype(jnp.float32), value_rows.astype(jnp.float32))
    mixed = mixed + own_prob.astype(jnp.float32)[..., None] * fresh_value.astype(jnp.float32)[:, None, :]
    return mixed.reshape(HEADS * HEAD_DIM).astype(jnp.bfloat16)

def reference(activations, gain, q_weight, kv_weight, o_weight, key_cache, value_cache, lengths):
    normed = normalize(activations, gain)
    query = jnp.dot(normed, q_weight, preferred_element_type=jnp.float32).astype(jnp.bfloat16)
    pairs = jnp.dot(normed, kv_weight, preferred_element_type=jnp.float32).astype(jnp.bfloat16)
    attended = lax.map(one_request, (query, pairs, key_cache, value_cache, lengths))
    return jnp.dot(attended, o_weight, preferred_element_type=jnp.float32).astype(jnp.bfloat16)
```

```python
import functools
import math

import jax
import jax.numpy as jnp
from jax import lax
from jax.experimental import pallas as pl
from jax.experimental.pallas import tpu as pltpu
from jax.sharding import PartitionSpec as P

HEADS = 128
KV_HEADS = 8
HEAD_DIM = 128
CACHE = 512
MESH = pl.DeviceIdType.MESH


rope_base = 500000.0
norm_eps = 1e-05


def rotate(vector, position):
    middle = vector.shape[-1] // 2
    offsets = jnp.arange(middle, dtype=jnp.float32)
    frequency = jnp.exp(offsets * (-2.0 * math.log(rope_base) / vector.shape[-1]))
    angles = position * frequency
    cosine = jnp.cos(angles)
    sine = jnp.sin(angles)
    leading = vector[..., :middle]
    trailing = vector[..., middle:]
    return jnp.concatenate(
        [leading * cosine - trailing * sine, trailing * cosine + leading * sine], axis=-1
    )


def normalize(activations, gain):
    widened = activations.astype(jnp.float32)
    inverse = lax.rsqrt(jnp.mean(widened * widened, axis=-1, keepdims=True) + norm_eps)
    return (widened * inverse * gain.astype(jnp.float32)).astype(jnp.bfloat16)


def shards(activations, gain, q_weight, kv_weight, o_weight, key_cache, value_cache, lengths):
    normed = normalize(activations, gain)
    piece = lax.all_gather(normed, "mp", axis=0, tiled=True)
    projected = jnp.concatenate(
        [
            jnp.dot(piece, q_weight, preferred_element_type=jnp.float32),
            jnp.dot(piece, kv_weight, preferred_element_type=jnp.float32),
        ],
        axis=1,
    ).astype(jnp.bfloat16)
    query_cols = q_weight.shape[1]
    query_all, pairs_all = (
        lax.all_to_all(projected[:, :query_cols], "mp", split_axis=0, concat_axis=1, tiled=True),
        lax.all_to_all(projected[:, query_cols:], "mp", split_axis=0, concat_axis=1, tiled=True),
    )
    requests = query_all.shape[0]
    per_group = HEADS // KV_HEADS
    scaling = 1.0 / math.sqrt(HEAD_DIM)
    position = lengths.astype(jnp.float32)
    query = rotate(
        query_all.astype(jnp.float32).reshape(requests, KV_HEADS, per_group, HEAD_DIM),
        position[:, None, None, None],
    ).astype(jnp.bfloat16)
    fresh_key = rotate(
        pairs_all[:, : KV_HEADS * HEAD_DIM]
        .astype(jnp.float32)
        .reshape(requests, KV_HEADS, HEAD_DIM),
        position[:, None, None],
    ).astype(jnp.bfloat16)
    fresh_value = pairs_all[:, KV_HEADS * HEAD_DIM :].reshape(requests, KV_HEADS, HEAD_DIM)
    scores = (
        jnp.einsum("rgqd,rgtd->rgqt", query, key_cache, preferred_element_type=jnp.float32)
        * scaling
    )
    visible = jnp.arange(CACHE, dtype=jnp.int32)[None, :] < lengths[:, None]
    scores = jnp.where(visible[:, None, None, :], scores, -1e30)
    own = (
        jnp.einsum("rgqd,rgd->rgq", query, fresh_key, preferred_element_type=jnp.float32) * scaling
    )
    highest = jnp.maximum(jnp.max(scores, axis=-1), own)
    weights = jnp.where(visible[:, None, None, :], jnp.exp(scores - highest[..., None]), 0.0)
    own_weight = jnp.exp(own - highest)
    denominator = jnp.sum(weights, axis=-1) + own_weight
    probs = (weights / denominator[..., None]).astype(jnp.bfloat16)
    own_prob = (own_weight / denominator).astype(jnp.bfloat16)
    mixed = jnp.einsum("rgqt,rgtd->rgqd", probs, value_cache, preferred_element_type=jnp.float32)
    mixed = (
        mixed
        + own_prob.astype(jnp.float32)[..., None] * fresh_value.astype(jnp.float32)[:, :, None, :]
    )
    attended = mixed.reshape(requests, HEADS * HEAD_DIM).astype(jnp.bfloat16)
    result = jnp.dot(
        lax.all_gather(attended, "mp", axis=0, tiled=True),
        o_weight,
        preferred_element_type=jnp.float32,
    )
    return result.astype(jnp.bfloat16)

def layout_of(mesh):
    row = mesh.devices.reshape(-1, mesh.shape["mp"])[0]
    chips = [tuple(d.coords) for d in row]
    cores = 1
    while cores < len(chips) and chips[cores] == chips[0]:
        cores += 1
    chips = chips[::cores]
    across = 1
    if len(chips) > 1:
        moved = [i for i in range(len(chips[0])) if chips[1][i] != chips[0][i]]
        fixed = [i for i in range(len(chips[0])) if i not in moved]
        while across < len(chips) and all(chips[across][i] == chips[0][i] for i in fixed):
            across += 1
    if len(chips) % across:
        across = 1
    return len(chips) // across, across, cores


def fused(
    dims,
    act_ref,
    gain_ref,
    cos_ref,
    sin_ref,
    len_ref,
    wq_ref,
    wkv_ref,
    wo_ref,
    kc_ref,
    vc_ref,
    out_ref,
    wbuf,
    kvbuf,
    kbuf,
    vbuf,
    x1,
    x2,
    acc,
    acc_kv,
    to_peers,
    from_peers,
    q_rows,
    a_rows,
    fresh,
    w_sem,
    kv_sem,
    cache_sem,
    send_sem,
    recv1,
    recv2,
    peer_send,
    peer_recv,
):
    lines, across, cores = dims
    devices = lines * across * cores
    rows = act_ref.shape[0]
    chunks = x1.shape[0]
    width = x1.shape[3]
    q_cols = wq_ref.shape[1]
    kv_cols = wkv_ref.shape[1]
    groups = chunks
    per_group = HEADS // groups
    hq = q_cols // HEAD_DIM
    hkv = kv_cols // HEAD_DIM
    me = lax.axis_index("mp")
    core = lax.rem(me, cores)
    col = lax.rem(me // cores, across)
    line = me // (cores * across)

    def index(l, a, k):
        return (l * across + a) * cores + k

    other_lines = [lax.rem(line + i, lines) for i in range(1, lines)]
    other_cols = [lax.rem(col + i, across) for i in range(1, across)]
    other_cores = [lax.rem(core + i, cores) for i in range(1, cores)]

    def weights(source, c):
        return pltpu.make_async_copy(
            source.at[pl.ds(pl.multiple_of(c * width, width), width), :], wbuf.at[c], w_sem.at[c]
        )

    kv_copy = pltpu.make_async_copy(wkv_ref, kvbuf, kv_sem.at[0])
    k_copy = pltpu.make_async_copy(kc_ref, kbuf, cache_sem.at[0])
    v_copy = pltpu.make_async_copy(vc_ref, vbuf, cache_sem.at[1])

    barrier = pltpu.get_barrier_semaphore()

    @pl.loop(1, devices)
    def _(i):
        pl.semaphore_signal(barrier, inc=1, device_id={"mp": lax.rem(me + i, devices)}, device_id_type=MESH)

    kv_copy.start()

    @pl.loop(0, chunks)
    def _(c):
        weights(wq_ref, c).start()

    k_copy.start()
    v_copy.start()

    widened = act_ref[...].astype(jnp.float32)
    inverse = lax.rsqrt(jnp.mean(widened * widened, axis=-1, keepdims=True) + norm_eps)
    for c in range(chunks):
        part = slice(c * width, (c + 1) * width)
        x1[c, me] = (
            act_ref[:, part].astype(jnp.float32) * inverse * gain_ref[:, part].astype(jnp.float32)
        ).astype(jnp.bfloat16)

    pl.semaphore_wait(barrier, devices - 1)

    def copies(x, recv, c):
        def remote(slot, block, target):
            return pltpu.make_async_remote_copy(
                src_ref=x.at[c, block],
                dst_ref=x.at[c, block],
                send_sem=send_sem.at[c, slot],
                recv_sem=recv.at[c, block],
                device_id={"mp": target},
                device_id_type=MESH,
            )

        first, second, third = [], [], []
        slot = 0
        for l in other_lines:
            first.append(remote(slot, me, index(l, col, core)))
            slot += 1
        for l in [line] + other_lines:
            block = index(l, col, core)
            group = []
            for a in other_cols:
                group.append(remote(slot, block, index(line, a, core)))
                slot += 1
            for k in other_cores:
                group.append(remote(slot, block, index(line, col, k)))
                slot += 1
            second.append((block, group))
        for a in other_cols:
            for l in [line] + other_lines:
                block = index(l, a, core)
                group = []
                for k in other_cores:
                    group.append(remote(slot, block, index(line, col, k)))
                    slot += 1
                third.append((block, group))
        return first, second, third

    def arrived(x, recv, c, block):
        pltpu.make_async_remote_copy(
            src_ref=x.at[c, block],
            dst_ref=x.at[c, block],
            send_sem=send_sem.at[c, 0],
            recv_sem=recv.at[c, block],
            device_id={"mp": lax.rem(me + 1, devices)},
            device_id_type=MESH,
        ).wait_recv()

    def send_own(x, recv, c):
        first, second, _ = copies(x, recv, c)
        for copy in first + second[0][1]:
            copy.start()

    def pass_on(x, recv, c):
        _, second, _ = copies(x, recv, c)
        for block, group in second[1:]:
            arrived(x, recv, c, block)
            for copy in group:
                copy.start()

    def finish(x, recv, c):
        _, _, third = copies(x, recv, c)
        for block, group in third:
            arrived(x, recv, c, block)
            for copy in group:
                copy.start()
        for k in other_cores:
            for a in [col] + other_cols:
                for l in [line] + other_lines:
                    arrived(x, recv, c, index(l, a, k))

    def drain(x, recv, c):
        first, second, third = copies(x, recv, c)
        for copy in first:
            copy.wait_send()
        for _, group in second + third:
            for copy in group:
                copy.wait_send()

    def gathered(x, c):
        block = x[c].astype(jnp.float32).reshape(devices * rows, width)
        return block.astype(jnp.bfloat16)

    @pl.loop(0, chunks)
    def _(c):
        send_own(x1, recv1, c)

    kv_copy.wait()
    pass_on(x1, recv1, 0)
    acc[...] = jnp.zeros_like(acc)
    acc_kv[...] = jnp.zeros_like(acc_kv)

    @pl.loop(0, chunks)
    def _(c):
        @pl.when(c + 1 < chunks)
        def _():
            pass_on(x1, recv1, c + 1)

        finish(x1, recv1, c)
        weights(wq_ref, c).wait()
        x = gathered(x1, c)
        acc[...] += jnp.dot(x, wbuf[c], preferred_element_type=jnp.float32)
        acc_kv[...] += jnp.dot(
            x,
            kvbuf[pl.ds(pl.multiple_of(c * width, width), width), :],
            preferred_element_type=jnp.float32,
        )
        weights(wo_ref, c).start()

    to_peers[:, :, :q_cols] = acc[...].reshape(devices, rows, q_cols).astype(jnp.bfloat16)
    to_peers[:, :, q_cols:] = acc_kv[...].reshape(devices, rows, kv_cols).astype(jnp.bfloat16)

    def exchange(i):
        target = lax.rem(me + i, devices)
        return pltpu.make_async_remote_copy(
            src_ref=to_peers.at[target],
            dst_ref=from_peers.at[me],
            send_sem=peer_send.at[i],
            recv_sem=peer_recv.at[me],
            device_id={"mp": target},
            device_id_type=MESH,
        )

    def exchanged(i):
        source = lax.rem(me + i, devices)
        return pltpu.make_async_remote_copy(
            src_ref=to_peers.at[source],
            dst_ref=from_peers.at[source],
            send_sem=peer_send.at[i],
            recv_sem=peer_recv.at[source],
            device_id={"mp": source},
            device_id_type=MESH,
        )

    @pl.loop(1, devices)
    def _(i):
        exchange(i).start()

    from_peers[me] = to_peers[me]

    @pl.loop(0, chunks)
    def _(c):
        drain(x1, recv1, c)

    k_copy.wait()
    v_copy.wait()

    @pl.loop(1, devices)
    def _(i):
        exchanged(i).wait_recv()

    @pl.loop(1, devices)
    def _(i):
        exchange(i).wait_send()

    cosine = cos_ref[...]
    sine = sin_ref[...]
    cosine_all = jnp.concatenate([cosine] * per_group, axis=0)
    sine_all = jnp.concatenate([sine] * per_group, axis=0)
    scaling = 1.0 / math.sqrt(HEAD_DIM)
    middle = HEAD_DIM // 2

    def turn(v, c, s):
        swapped = jnp.concatenate([v[:, middle:], v[:, :middle]], axis=1)
        return (v * c + swapped * s).astype(jnp.bfloat16).astype(jnp.float32)

    def pair_head(j):
        if hkv == 1:
            return from_peers[j, :, q_cols:].astype(jnp.float32)
        at = pl.multiple_of(q_cols + lax.rem(j, hkv) * HEAD_DIM, HEAD_DIM)
        return from_peers[j // hkv, :, pl.ds(at, HEAD_DIM)].astype(jnp.float32)

    @pl.loop(0, groups)
    def _(g):
        heads = []
        for h in range(per_group):
            owner = g * (per_group // hq) + h // hq
            at = (h % hq) * HEAD_DIM
            heads.append(from_peers[owner, :, at : at + HEAD_DIM].astype(jnp.float32))
        q_rows[...] = turn(jnp.concatenate(heads, axis=0), cosine_all, sine_all)
        fresh[0:rows, :] = turn(pair_head(g), cosine, sine)
        fresh[rows : 2 * rows, :] = pair_head(groups + g)
        for r in range(rows):
            query = q_rows[pl.ds(r, per_group, stride=rows), :]
            new_key = fresh[r : r + 1, :]
            new_value = fresh[rows + r : rows + r + 1, :]
            scores = (
                lax.dot_general(
                    query.astype(jnp.bfloat16),
                    kbuf[r, g],
                    (((1,), (1,)), ((), ())),
                    preferred_element_type=jnp.float32,
                )
                * scaling
            )
            visible = lax.broadcasted_iota(jnp.int32, scores.shape, 1) < len_ref[r]
            scores = jnp.where(visible, scores, -1e30)
            own = jnp.sum(query * new_key, axis=-1, keepdims=True) * scaling
            highest = jnp.maximum(jnp.max(scores, axis=-1, keepdims=True), own)
            weight = jnp.where(visible, jnp.exp(scores - highest), 0.0)
            own_weight = jnp.exp(own - highest)
            denominator = jnp.sum(weight, axis=-1, keepdims=True) + own_weight
            probs = (weight / denominator).astype(jnp.bfloat16)
            own_prob = (own_weight / denominator).astype(jnp.bfloat16).astype(jnp.float32)
            mixed = jnp.dot(probs, vbuf[r, g], preferred_element_type=jnp.float32)
            a_rows[pl.ds(r, per_group, stride=rows), :] = mixed + own_prob * new_value
        for h in range(per_group):
            x2[g, me, :, h * HEAD_DIM : (h + 1) * HEAD_DIM] = a_rows[
                h * rows : (h + 1) * rows, :
            ].astype(jnp.bfloat16)
        send_own(x2, recv2, g)

    pass_on(x2, recv2, 0)
    acc[...] = jnp.zeros_like(acc)

    @pl.loop(0, chunks)
    def _(c):
        @pl.when(c + 1 < chunks)
        def _():
            pass_on(x2, recv2, c + 1)

        finish(x2, recv2, c)
        weights(wo_ref, c).wait()
        acc[...] += jnp.dot(gathered(x2, c), wbuf[c], preferred_element_type=jnp.float32)

    out_ref[...] = acc[...].astype(jnp.bfloat16)

    @pl.loop(0, chunks)
    def _(c):
        drain(x2, recv2, c)


def fused_shards(
    dims, activations, gain, q_weight, kv_weight, o_weight, key_cache, value_cache, lengths
):
    devices = dims[0] * dims[1] * dims[2]
    rows, features = activations.shape
    q_cols = q_weight.shape[1]
    kv_cols = kv_weight.shape[1]
    chunks = KV_HEADS
    width = features // chunks
    middle = HEAD_DIM // 2
    offsets = jnp.arange(middle, dtype=jnp.float32)
    frequency = jnp.exp(offsets * (-2.0 * math.log(rope_base) / HEAD_DIM))
    angles = lengths.astype(jnp.float32)[:, None] * frequency
    cosine = jnp.cos(angles)
    sine = jnp.sin(angles)
    sends = devices - 1
    vmem = pl.BlockSpec(memory_space=pltpu.VMEM)
    hbm = pl.BlockSpec(memory_space=pl.ANY)
    dma = pltpu.SemaphoreType.DMA
    return pl.pallas_call(
        functools.partial(fused, dims),
        out_shape=jax.ShapeDtypeStruct((devices * rows, o_weight.shape[1]), jnp.bfloat16),
        in_specs=[vmem] * 4 + [pl.BlockSpec(memory_space=pltpu.SMEM)] + [hbm] * 5,
        out_specs=vmem,
        scratch_shapes=[
            pltpu.VMEM((chunks, width, q_cols), jnp.bfloat16),
            pltpu.VMEM(kv_weight.shape, jnp.bfloat16),
            pltpu.VMEM(key_cache.shape, jnp.bfloat16),
            pltpu.VMEM(value_cache.shape, jnp.bfloat16),
            pltpu.VMEM((chunks, devices, rows, width), jnp.bfloat16),
            pltpu.VMEM((chunks, devices, rows, width), jnp.bfloat16),
            pltpu.VMEM((devices * rows, q_cols), jnp.float32),
            pltpu.VMEM((devices * rows, kv_cols), jnp.float32),
            pltpu.VMEM((devices, rows, q_cols + kv_cols), jnp.bfloat16),
            pltpu.VMEM((devices, rows, q_cols + kv_cols), jnp.bfloat16),
            pltpu.VMEM((HEADS // KV_HEADS * rows, HEAD_DIM), jnp.float32),
            pltpu.VMEM((HEADS // KV_HEADS * rows, HEAD_DIM), jnp.float32),
            pltpu.VMEM((2 * rows, HEAD_DIM), jnp.float32),
            dma((chunks,)),
            dma((1,)),
            dma((2,)),
            dma((chunks, sends)),
            dma((chunks, devices)),
            dma((chunks, devices)),
            dma((devices,)),
            dma((devices,)),
        ],
        compiler_params=pltpu.CompilerParams(
            collective_id=0, has_side_effects=True, vmem_limit_bytes=62 * 1024 * 1024
        ),
    )(
        activations,
        gain.reshape(1, features),
        jnp.concatenate([cosine, cosine], axis=1),
        jnp.concatenate([-sine, sine], axis=1),
        lengths,
        q_weight,
        kv_weight,
        o_weight,
        key_cache,
        value_cache,
    )


def fits(mesh):
    devices = mesh.shape["mp"]
    per_group = HEADS // KV_HEADS
    heads = HEADS // devices if HEADS % devices == 0 else 0
    pairs = 2 * KV_HEADS // devices if 2 * KV_HEADS % devices == 0 else 0
    return heads > 0 and pairs > 0 and per_group % heads == 0


def solution(mesh):
    placed = (
        P(("groups", "mp"), None),
        P(),
        P(None, "mp"),
        P(None, "mp"),
        P(None, "mp"),
        P(("groups", "mp"), None, None, None),
        P(("groups", "mp"), None, None, None),
        P(("groups", "mp")),
    )
    body = functools.partial(fused_shards, layout_of(mesh)) if fits(mesh) else shards
    return jax.shard_map(
        body, mesh=mesh, in_specs=placed, out_specs=P("groups", "mp"), check_vma=False
    )
```

```python
import functools
import math

import jax
import jax.numpy as jnp
from jax import lax
from jax.experimental import pallas as pl
from jax.experimental.pallas import tpu as pltpu
from jax.sharding import PartitionSpec as P

HEADS = 128
KV_HEADS = 8
HEAD_DIM = 128
CACHE = 512
MESH = pl.DeviceIdType.MESH


rope_base = 500000.0
norm_eps = 1e-05


def rotate(vector, position):
    middle = vector.shape[-1] // 2
    offsets = jnp.arange(middle, dtype=jnp.float32)
    frequency = jnp.exp(offsets * (-2.0 * math.log(rope_base) / vector.shape[-1]))
    angles = position * frequency
    cosine = jnp.cos(angles)
    sine = jnp.sin(angles)
    leading = vector[..., :middle]
    trailing = vector[..., middle:]
    return jnp.concatenate(
        [leading * cosine - trailing * sine, trailing * cosine + leading * sine], axis=-1
    )


def normalize(activations, gain):
    widened = activations.astype(jnp.float32)
    inverse = lax.rsqrt(jnp.mean(widened * widened, axis=-1, keepdims=True) + norm_eps)
    return (widened * inverse * gain.astype(jnp.float32)).astype(jnp.bfloat16)


def shards(activations, gain, q_weight, kv_weight, o_weight, key_cache, value_cache, lengths):
    normed = normalize(activations, gain)
    piece = lax.all_gather(normed, "mp", axis=0, tiled=True)
    projected = jnp.concatenate(
        [
            jnp.dot(piece, q_weight, preferred_element_type=jnp.float32),
            jnp.dot(piece, kv_weight, preferred_element_type=jnp.float32),
        ],
        axis=1,
    ).astype(jnp.bfloat16)
    query_cols = q_weight.shape[1]
    query_all, pairs_all = (
        lax.all_to_all(projected[:, :query_cols], "mp", split_axis=0, concat_axis=1, tiled=True),
        lax.all_to_all(projected[:, query_cols:], "mp", split_axis=0, concat_axis=1, tiled=True),
    )
    requests = query_all.shape[0]
    per_group = HEADS // KV_HEADS
    scaling = 1.0 / math.sqrt(HEAD_DIM)
    position = lengths.astype(jnp.float32)
    query = rotate(
        query_all.astype(jnp.float32).reshape(requests, KV_HEADS, per_group, HEAD_DIM),
        position[:, None, None, None],
    ).astype(jnp.bfloat16)
    fresh_key = rotate(
        pairs_all[:, : KV_HEADS * HEAD_DIM]
        .astype(jnp.float32)
        .reshape(requests, KV_HEADS, HEAD_DIM),
        position[:, None, None],
    ).astype(jnp.bfloat16)
    fresh_value = pairs_all[:, KV_HEADS * HEAD_DIM :].reshape(requests, KV_HEADS, HEAD_DIM)
    scores = (
        jnp.einsum("rgqd,rgtd->rgqt", query, key_cache, preferred_element_type=jnp.float32)
        * scaling
    )
    visible = jnp.arange(CACHE, dtype=jnp.int32)[None, :] < lengths[:, None]
    scores = jnp.where(visible[:, None, None, :], scores, -1e30)
    own = (
        jnp.einsum("rgqd,rgd->rgq", query, fresh_key, preferred_element_type=jnp.float32) * scaling
    )
    highest = jnp.maximum(jnp.max(scores, axis=-1), own)
    weights = jnp.where(visible[:, None, None, :], jnp.exp(scores - highest[..., None]), 0.0)
    own_weight = jnp.exp(own - highest)
    denominator = jnp.sum(weights, axis=-1) + own_weight
    probs = (weights / denominator[..., None]).astype(jnp.bfloat16)
    own_prob = (own_weight / denominator).astype(jnp.bfloat16)
    mixed = jnp.einsum("rgqt,rgtd->rgqd", probs, value_cache, preferred_element_type=jnp.float32)
    mixed = (
        mixed
        + own_prob.astype(jnp.float32)[..., None] * fresh_value.astype(jnp.float32)[:, :, None, :]
    )
    attended = mixed.reshape(requests, HEADS * HEAD_DIM).astype(jnp.bfloat16)
    result = jnp.dot(
        lax.all_gather(attended, "mp", axis=0, tiled=True),
        o_weight,
        preferred_element_type=jnp.float32,
    )
    return result.astype(jnp.bfloat16)

def layout_of(mesh):
    row = mesh.devices.reshape(-1, mesh.shape["mp"])[0]
    chips = [tuple(d.coords) for d in row]
    cores = 1
    while cores < len(chips) and chips[cores] == chips[0]:
        cores += 1
    chips = chips[::cores]
    across = 1
    if len(chips) > 1:
        moved = [i for i in range(len(chips[0])) if chips[1][i] != chips[0][i]]
        fixed = [i for i in range(len(chips[0])) if i not in moved]
        while across < len(chips) and all(chips[across][i] == chips[0][i] for i in fixed):
            across += 1
    if len(chips) % across:
        across = 1
    return len(chips) // across, across, cores


def fused(
    dims,
    act_ref,
    gain_ref,
    len_ref,
    wq_ref,
    wkv_ref,
    wo_ref,
    kc_ref,
    vc_ref,
    out_ref,
    wbuf,
    kvbuf,
    kbuf,
    vbuf,
    x1,
    x2,
    acc,
    acc_kv,
    to_peers,
    from_peers,
    q_rows,
    a_rows,
    fresh,
    tables,
    w_sem,
    kv_sem,
    cache_sem,
    send_sem,
    recv1,
    recv2,
    peer_send,
    peer_recv,
):
    lines, across, cores = dims
    devices = lines * across * cores
    rows = act_ref.shape[0]
    chunks = x1.shape[0]
    width = x1.shape[3]
    q_cols = wq_ref.shape[1]
    kv_cols = wkv_ref.shape[1]
    groups = chunks
    per_group = HEADS // groups
    hq = q_cols // HEAD_DIM
    hkv = kv_cols // HEAD_DIM
    me = lax.axis_index("mp")
    core = lax.rem(me, cores)
    col = lax.rem(me // cores, across)
    line = me // (cores * across)

    def index(l, a, k):
        return (l * across + a) * cores + k

    other_lines = [lax.rem(line + i, lines) for i in range(1, lines)]
    other_cols = [lax.rem(col + i, across) for i in range(1, across)]
    other_cores = [lax.rem(core + i, cores) for i in range(1, cores)]

    def weights(source, c):
        return pltpu.make_async_copy(
            source.at[pl.ds(pl.multiple_of(c * width, width), width), :], wbuf.at[c], w_sem.at[c]
        )

    kv_copy = pltpu.make_async_copy(wkv_ref, kvbuf, kv_sem.at[0])
    k_copy = pltpu.make_async_copy(kc_ref, kbuf, cache_sem.at[0])
    v_copy = pltpu.make_async_copy(vc_ref, vbuf, cache_sem.at[1])

    barrier = pltpu.get_barrier_semaphore()

    @pl.loop(1, devices)
    def _(i):
        pl.semaphore_signal(barrier, inc=1, device_id={"mp": lax.rem(me + i, devices)}, device_id_type=MESH)

    kv_copy.start()

    @pl.loop(0, chunks)
    def _(c):
        weights(wq_ref, c).start()

    k_copy.start()
    v_copy.start()

    widened = act_ref[...].astype(jnp.float32)
    inverse = lax.rsqrt(jnp.mean(widened * widened, axis=-1, keepdims=True) + norm_eps)
    for c in range(chunks):
        part = slice(c * width, (c + 1) * width)
        x1[c, me] = (
            act_ref[:, part].astype(jnp.float32) * inverse * gain_ref[part].astype(jnp.float32)
        ).astype(jnp.bfloat16)

    pl.semaphore_wait(barrier, devices - 1)

    def copies(x, recv, c):
        def remote(slot, block, target):
            return pltpu.make_async_remote_copy(
                src_ref=x.at[c, block],
                dst_ref=x.at[c, block],
                send_sem=send_sem.at[c, slot],
                recv_sem=recv.at[c, block],
                device_id={"mp": target},
                device_id_type=MESH,
            )

        first, second, third = [], [], []
        slot = 0
        for l in other_lines:
            first.append(remote(slot, me, index(l, col, core)))
            slot += 1
        for l in [line] + other_lines:
            block = index(l, col, core)
            group = []
            for a in other_cols:
                group.append(remote(slot, block, index(line, a, core)))
                slot += 1
            for k in other_cores:
                group.append(remote(slot, block, index(line, col, k)))
                slot += 1
            second.append((block, group))
        for a in other_cols:
            for l in [line] + other_lines:
                block = index(l, a, core)
                group = []
                for k in other_cores:
                    group.append(remote(slot, block, index(line, col, k)))
                    slot += 1
                third.append((block, group))
        return first, second, third

    def arrived(x, recv, c, block):
        pltpu.make_async_remote_copy(
            src_ref=x.at[c, block],
            dst_ref=x.at[c, block],
            send_sem=send_sem.at[c, 0],
            recv_sem=recv.at[c, block],
            device_id={"mp": lax.rem(me + 1, devices)},
            device_id_type=MESH,
        ).wait_recv()

    def send_own(x, recv, c):
        first, second, _ = copies(x, recv, c)
        for copy in first + second[0][1]:
            copy.start()

    def pass_on(x, recv, c):
        _, second, _ = copies(x, recv, c)
        for block, group in second[1:]:
            arrived(x, recv, c, block)
            for copy in group:
                copy.start()

    def finish(x, recv, c):
        _, _, third = copies(x, recv, c)
        for block, group in third:
            arrived(x, recv, c, block)
            for copy in group:
                copy.start()

    def settle(x, recv, c):
        for k in other_cores:
            for a in [col] + other_cols:
                for l in [line] + other_lines:
                    arrived(x, recv, c, index(l, a, k))

    def drain(x, recv, c):
        first, second, third = copies(x, recv, c)
        for copy in first:
            copy.wait_send()
        for _, group in second + third:
            for copy in group:
                copy.wait_send()

    def gathered(x, c):
        block = x[c].astype(jnp.float32).reshape(devices * rows, width)
        return block.astype(jnp.bfloat16)

    @pl.loop(0, chunks)
    def _(c):
        send_own(x1, recv1, c)

    middle = HEAD_DIM // 2
    lane = lax.broadcasted_iota(jnp.int32, (rows, HEAD_DIM), 1)
    which = lax.broadcasted_iota(jnp.int32, (rows, HEAD_DIM), 0)
    position = jnp.zeros((rows, HEAD_DIM), jnp.float32)
    for r in range(rows):
        position = jnp.where(which == r, len_ref[r].astype(jnp.float32), position)
    offsets = jnp.where(lane < middle, lane, lane - middle).astype(jnp.float32)
    angles = position * jnp.exp(offsets * (-2.0 * math.log(rope_base) / HEAD_DIM))
    sine = jnp.sin(angles)
    tables[0] = jnp.concatenate([jnp.cos(angles)] * per_group, axis=0)
    tables[1] = jnp.concatenate([jnp.where(lane < middle, -sine, sine)] * per_group, axis=0)

    kv_copy.wait()
    acc[...] = jnp.zeros_like(acc)
    acc_kv[...] = jnp.zeros_like(acc_kv)
    early = min(2, chunks)
    for c in range(early):
        pass_on(x1, recv1, c)
    finish(x1, recv1, 0)

    @pl.loop(0, chunks)
    def _(c):
        @pl.when(c + early < chunks)
        def _():
            pass_on(x1, recv1, c + early)

        @pl.when(c + 1 < chunks)
        def _():
            finish(x1, recv1, c + 1)

        settle(x1, recv1, c)
        weights(wq_ref, c).wait()
        x = gathered(x1, c)
        acc[...] += jnp.dot(x, wbuf[c], preferred_element_type=jnp.float32)
        acc_kv[...] += jnp.dot(
            x,
            kvbuf[pl.ds(pl.multiple_of(c * width, width), width), :],
            preferred_element_type=jnp.float32,
        )
        weights(wo_ref, c).start()

    to_peers[:, :, :q_cols] = acc[...].reshape(devices, rows, q_cols).astype(jnp.bfloat16)
    to_peers[:, :, q_cols:] = acc_kv[...].reshape(devices, rows, kv_cols).astype(jnp.bfloat16)

    def exchange(i):
        target = lax.rem(me + i, devices)
        return pltpu.make_async_remote_copy(
            src_ref=to_peers.at[target],
            dst_ref=from_peers.at[me],
            send_sem=peer_send.at[i],
            recv_sem=peer_recv.at[me],
            device_id={"mp": target},
            device_id_type=MESH,
        )

    def exchanged(i):
        source = lax.rem(me + i, devices)
        return pltpu.make_async_remote_copy(
            src_ref=to_peers.at[source],
            dst_ref=from_peers.at[source],
            send_sem=peer_send.at[i],
            recv_sem=peer_recv.at[source],
            device_id={"mp": source},
            device_id_type=MESH,
        )

    @pl.loop(1, devices)
    def _(i):
        exchange(i).start()

    from_peers[me] = to_peers[me]

    @pl.loop(0, chunks)
    def _(c):
        drain(x1, recv1, c)

    k_copy.wait()
    v_copy.wait()

    @pl.loop(1, devices)
    def _(i):
        exchanged(i).wait_recv()

    @pl.loop(1, devices)
    def _(i):
        exchange(i).wait_send()

    scaling = 1.0 / math.sqrt(HEAD_DIM)

    def turn(v, c, s):
        swapped = jnp.concatenate([v[:, middle:], v[:, :middle]], axis=1)
        return (v * c + swapped * s).astype(jnp.bfloat16).astype(jnp.float32)

    def pair_head(j):
        if hkv == 1:
            return from_peers[j, :, q_cols:].astype(jnp.float32)
        at = pl.multiple_of(q_cols + lax.rem(j, hkv) * HEAD_DIM, HEAD_DIM)
        return from_peers[j // hkv, :, pl.ds(at, HEAD_DIM)].astype(jnp.float32)

    passing = min(3, chunks)
    finishing = min(5, chunks)

    @pl.loop(0, groups)
    def _(g):
        @pl.when(g >= passing)
        def _():
            pass_on(x2, recv2, g - passing)

        @pl.when(g >= finishing)
        def _():
            finish(x2, recv2, g - finishing)

        heads = []
        for h in range(per_group):
            owner = g * (per_group // hq) + h // hq
            at = (h % hq) * HEAD_DIM
            heads.append(from_peers[owner, :, at : at + HEAD_DIM].astype(jnp.float32))
        q_rows[...] = turn(jnp.concatenate(heads, axis=0), tables[0], tables[1])
        fresh[0:rows, :] = turn(pair_head(g), tables[0, 0:rows, :], tables[1, 0:rows, :])
        fresh[rows : 2 * rows, :] = pair_head(groups + g)
        slots = kbuf.shape[2]
        slot = lax.broadcasted_iota(jnp.int32, (per_group, slots), 1)
        scores, own = [], []
        for r in range(rows):
            query = q_rows[pl.ds(r, per_group, stride=rows), :]
            own.append(jnp.sum(query * fresh[r : r + 1, :], axis=-1, keepdims=True))
            part = lax.dot_general(
                query.astype(jnp.bfloat16),
                kbuf[r, g],
                (((1,), (1,)), ((), ())),
                preferred_element_type=jnp.float32,
            )
            scores.append(jnp.where(slot < len_ref[r], part * scaling, -1e30))
        scores = jnp.concatenate(scores, axis=0)
        own = jnp.concatenate(own, axis=0) * scaling
        highest = jnp.maximum(jnp.max(scores, axis=-1, keepdims=True), own)
        weight = jnp.exp(scores - highest)
        own_weight = jnp.exp(own - highest)
        scale = 1.0 / (jnp.sum(weight, axis=-1, keepdims=True) + own_weight)
        probs = (weight * scale).astype(jnp.bfloat16)
        own_prob = (own_weight * scale).astype(jnp.bfloat16).astype(jnp.float32)
        mixed = []
        for r in range(rows):
            at = slice(r * per_group, (r + 1) * per_group)
            mixed.append(
                jnp.dot(probs[at], vbuf[r, g], preferred_element_type=jnp.float32)
                + own_prob[at] * fresh[rows + r : rows + r + 1, :]
            )
        for r in range(rows):
            a_rows[pl.ds(r, per_group, stride=rows), :] = mixed[r]
        for h in range(per_group):
            x2[g, me, :, h * HEAD_DIM : (h + 1) * HEAD_DIM] = a_rows[
                h * rows : (h + 1) * rows, :
            ].astype(jnp.bfloat16)
        send_own(x2, recv2, g)

    acc[...] = jnp.zeros_like(acc)

    @pl.loop(0, chunks)
    def _(c):
        @pl.when(c + chunks - passing < chunks)
        def _():
            pass_on(x2, recv2, c + chunks - passing)

        @pl.when(c + chunks - finishing < chunks)
        def _():
            finish(x2, recv2, c + chunks - finishing)

        settle(x2, recv2, c)
        weights(wo_ref, c).wait()
        acc[...] += jnp.dot(gathered(x2, c), wbuf[c], preferred_element_type=jnp.float32)

    out_ref[...] = acc[...].astype(jnp.bfloat16)

    @pl.loop(0, chunks)
    def _(c):
        drain(x2, recv2, c)


def fused_shards(
    dims, activations, gain, q_weight, kv_weight, o_weight, key_cache, value_cache, lengths
):
    devices = dims[0] * dims[1] * dims[2]
    rows, features = activations.shape
    q_cols = q_weight.shape[1]
    kv_cols = kv_weight.shape[1]
    chunks = KV_HEADS
    width = features // chunks
    sends = devices - 1
    vmem = pl.BlockSpec(memory_space=pltpu.VMEM)
    hbm = pl.BlockSpec(memory_space=pl.ANY)
    dma = pltpu.SemaphoreType.DMA
    return pl.pallas_call(
        functools.partial(fused, dims),
        out_shape=jax.ShapeDtypeStruct((devices * rows, o_weight.shape[1]), jnp.bfloat16),
        in_specs=[vmem] * 2 + [pl.BlockSpec(memory_space=pltpu.SMEM)] + [hbm] * 5,
        out_specs=vmem,
        scratch_shapes=[
            pltpu.VMEM((chunks, width, q_cols), jnp.bfloat16),
            pltpu.VMEM(kv_weight.shape, jnp.bfloat16),
            pltpu.VMEM(key_cache.shape, jnp.bfloat16),
            pltpu.VMEM(value_cache.shape, jnp.bfloat16),
            pltpu.VMEM((chunks, devices, rows, width), jnp.bfloat16),
            pltpu.VMEM((chunks, devices, rows, width), jnp.bfloat16),
            pltpu.VMEM((devices * rows, q_cols), jnp.float32),
            pltpu.VMEM((devices * rows, kv_cols), jnp.float32),
            pltpu.VMEM((devices, rows, q_cols + kv_cols), jnp.bfloat16),
            pltpu.VMEM((devices, rows, q_cols + kv_cols), jnp.bfloat16),
            pltpu.VMEM((HEADS // KV_HEADS * rows, HEAD_DIM), jnp.float32),
            pltpu.VMEM((HEADS // KV_HEADS * rows, HEAD_DIM), jnp.float32),
            pltpu.VMEM((2 * rows, HEAD_DIM), jnp.float32),
            pltpu.VMEM((2, HEADS // KV_HEADS * rows, HEAD_DIM), jnp.float32),
            dma((chunks,)),
            dma((1,)),
            dma((2,)),
            dma((chunks, sends)),
            dma((chunks, devices)),
            dma((chunks, devices)),
            dma((devices,)),
            dma((devices,)),
        ],
        compiler_params=pltpu.CompilerParams(
            collective_id=0, has_side_effects=True, vmem_limit_bytes=62 * 1024 * 1024
        ),
    )(
        activations,
        gain,
        lengths,
        q_weight,
        kv_weight,
        o_weight,
        key_cache,
        value_cache,
    )


def fits(mesh):
    devices = mesh.shape["mp"]
    per_group = HEADS // KV_HEADS
    heads = HEADS // devices if HEADS % devices == 0 else 0
    pairs = 2 * KV_HEADS // devices if 2 * KV_HEADS % devices == 0 else 0
    return heads > 0 and pairs > 0 and per_group % heads == 0


def solution(mesh):
    placed = (
        P(("groups", "mp"), None),
        P(),
        P(None, "mp"),
        P(None, "mp"),
        P(None, "mp"),
        P(("groups", "mp"), None, None, None),
        P(("groups", "mp"), None, None, None),
        P(("groups", "mp")),
    )
    body = functools.partial(fused_shards, layout_of(mesh)) if fits(mesh) else shards
    return jax.shard_map(
        body, mesh=mesh, in_specs=placed, out_specs=P("groups", "mp"), check_vma=False
    )
```

```python
import functools
import math

import jax
import jax.numpy as jnp
from jax import lax
from jax.experimental import pallas as pl
from jax.experimental.pallas import tpu as pltpu
from jax.sharding import PartitionSpec as P

HEADS = 128
KV_HEADS = 8
HEAD_DIM = 128
CACHE = 512
MESH = pl.DeviceIdType.MESH


rope_base = 500000.0
norm_eps = 1e-05


def rotate(vector, position):
    middle = vector.shape[-1] // 2
    offsets = jnp.arange(middle, dtype=jnp.float32)
    frequency = jnp.exp(offsets * (-2.0 * math.log(rope_base) / vector.shape[-1]))
    angles = position * frequency
    cosine = jnp.cos(angles)
    sine = jnp.sin(angles)
    leading = vector[..., :middle]
    trailing = vector[..., middle:]
    return jnp.concatenate(
        [leading * cosine - trailing * sine, trailing * cosine + leading * sine], axis=-1
    )


def normalize(activations, gain):
    widened = activations.astype(jnp.float32)
    inverse = lax.rsqrt(jnp.mean(widened * widened, axis=-1, keepdims=True) + norm_eps)
    return (widened * inverse * gain.astype(jnp.float32)).astype(jnp.bfloat16)


def shards(activations, gain, q_weight, kv_weight, o_weight, key_cache, value_cache, lengths):
    normed = normalize(activations, gain)
    piece = lax.all_gather(normed, "mp", axis=0, tiled=True)
    projected = jnp.concatenate(
        [
            jnp.dot(piece, q_weight, preferred_element_type=jnp.float32),
            jnp.dot(piece, kv_weight, preferred_element_type=jnp.float32),
        ],
        axis=1,
    ).astype(jnp.bfloat16)
    query_cols = q_weight.shape[1]
    query_all, pairs_all = (
        lax.all_to_all(projected[:, :query_cols], "mp", split_axis=0, concat_axis=1, tiled=True),
        lax.all_to_all(projected[:, query_cols:], "mp", split_axis=0, concat_axis=1, tiled=True),
    )
    requests = query_all.shape[0]
    per_group = HEADS // KV_HEADS
    scaling = 1.0 / math.sqrt(HEAD_DIM)
    position = lengths.astype(jnp.float32)
    query = rotate(
        query_all.astype(jnp.float32).reshape(requests, KV_HEADS, per_group, HEAD_DIM),
        position[:, None, None, None],
    ).astype(jnp.bfloat16)
    fresh_key = rotate(
        pairs_all[:, : KV_HEADS * HEAD_DIM]
        .astype(jnp.float32)
        .reshape(requests, KV_HEADS, HEAD_DIM),
        position[:, None, None],
    ).astype(jnp.bfloat16)
    fresh_value = pairs_all[:, KV_HEADS * HEAD_DIM :].reshape(requests, KV_HEADS, HEAD_DIM)
    scores = (
        jnp.einsum("rgqd,rgtd->rgqt", query, key_cache, preferred_element_type=jnp.float32)
        * scaling
    )
    visible = jnp.arange(CACHE, dtype=jnp.int32)[None, :] < lengths[:, None]
    scores = jnp.where(visible[:, None, None, :], scores, -1e30)
    own = (
        jnp.einsum("rgqd,rgd->rgq", query, fresh_key, preferred_element_type=jnp.float32) * scaling
    )
    highest = jnp.maximum(jnp.max(scores, axis=-1), own)
    weights = jnp.where(visible[:, None, None, :], jnp.exp(scores - highest[..., None]), 0.0)
    own_weight = jnp.exp(own - highest)
    denominator = jnp.sum(weights, axis=-1) + own_weight
    probs = (weights / denominator[..., None]).astype(jnp.bfloat16)
    own_prob = (own_weight / denominator).astype(jnp.bfloat16)
    mixed = jnp.einsum("rgqt,rgtd->rgqd", probs, value_cache, preferred_element_type=jnp.float32)
    mixed = (
        mixed
        + own_prob.astype(jnp.float32)[..., None] * fresh_value.astype(jnp.float32)[:, :, None, :]
    )
    attended = mixed.reshape(requests, HEADS * HEAD_DIM).astype(jnp.bfloat16)
    result = jnp.dot(
        lax.all_gather(attended, "mp", axis=0, tiled=True),
        o_weight,
        preferred_element_type=jnp.float32,
    )
    return result.astype(jnp.bfloat16)

def layout_of(mesh):
    row = mesh.devices.reshape(-1, mesh.shape["mp"])[0]
    chips = [tuple(d.coords) for d in row]
    cores = 1
    while cores < len(chips) and chips[cores] == chips[0]:
        cores += 1
    chips = chips[::cores]
    across = 1
    if len(chips) > 1:
        moved = [i for i in range(len(chips[0])) if chips[1][i] != chips[0][i]]
        fixed = [i for i in range(len(chips[0])) if i not in moved]
        while across < len(chips) and all(chips[across][i] == chips[0][i] for i in fixed):
            across += 1
    if len(chips) % across:
        across = 1
    return len(chips) // across, across, cores


def fused(
    dims,
    act_ref,
    gain_ref,
    len_ref,
    wq_ref,
    wkv_ref,
    wo_ref,
    kc_ref,
    vc_ref,
    out_ref,
    wbuf,
    kvbuf,
    kbuf,
    vbuf,
    x1,
    x2,
    acc,
    acc_kv,
    to_peers,
    from_peers,
    q_rows,
    a_rows,
    fresh,
    tables,
    w_sem,
    kv_sem,
    cache_sem,
    send_sem,
    recv1,
    recv2,
    peer_send,
    peer_recv,
):
    lines, across, cores = dims
    devices = lines * across * cores
    rows = act_ref.shape[0]
    chunks = x1.shape[0]
    width = x1.shape[3]
    q_cols = wq_ref.shape[1]
    kv_cols = wkv_ref.shape[1]
    groups = chunks
    per_group = HEADS // groups
    hq = q_cols // HEAD_DIM
    hkv = kv_cols // HEAD_DIM
    me = lax.axis_index("mp")
    core = lax.rem(me, cores)
    col = lax.rem(me // cores, across)
    line = me // (cores * across)

    def index(l, a, k):
        return (l * across + a) * cores + k

    def place(l, a, k):
        return (k * across + a) * lines + l

    def place_of(device):
        rest = device // cores
        return place(rest // across, lax.rem(rest, across), lax.rem(device, cores))

    mine = place(line, col, core)
    other_lines = [lax.rem(line + i, lines) for i in range(1, lines)]
    other_cols = [lax.rem(col + i, across) for i in range(1, across)]
    other_cores = [lax.rem(core + i, cores) for i in range(1, cores)]

    def weights(source, c):
        return pltpu.make_async_copy(
            source.at[pl.ds(pl.multiple_of(c * width, width), width), :], wbuf.at[c], w_sem.at[c]
        )

    kv_copy = pltpu.make_async_copy(wkv_ref, kvbuf, kv_sem.at[0])
    k_copy = pltpu.make_async_copy(kc_ref, kbuf, cache_sem.at[0])
    v_copy = pltpu.make_async_copy(vc_ref, vbuf, cache_sem.at[1])

    barrier = pltpu.get_barrier_semaphore()

    @pl.loop(1, devices)
    def _(i):
        pl.semaphore_signal(barrier, inc=1, device_id={"mp": lax.rem(me + i, devices)}, device_id_type=MESH)

    kv_copy.start()

    @pl.loop(0, chunks)
    def _(c):
        weights(wq_ref, c).start()

    k_copy.start()
    v_copy.start()

    widened = act_ref[...].astype(jnp.float32)
    inverse = lax.rsqrt(jnp.mean(widened * widened, axis=-1, keepdims=True) + norm_eps)
    for c in range(chunks):
        part = slice(c * width, (c + 1) * width)
        x1[c, mine] = (
            act_ref[:, part].astype(jnp.float32) * inverse * gain_ref[part].astype(jnp.float32)
        ).astype(jnp.bfloat16)

    pl.semaphore_wait(barrier, devices - 1)

    def remote(x, recv, c, at, size, slot, arrival, target):
        return pltpu.make_async_remote_copy(
            src_ref=x.at[c, pl.ds(at, size)],
            dst_ref=x.at[c, pl.ds(at, size)],
            send_sem=send_sem.at[c, slot],
            recv_sem=recv.at[c, arrival],
            device_id={"mp": target},
            device_id_type=MESH,
        )

    def to_lines(x, recv, c):
        return [
            remote(x, recv, c, mine, 1, i, line, index(l, col, core))
            for i, l in enumerate(other_lines)
        ]

    def to_cols(x, recv, c):
        at = place(0, col, core)
        return [
            remote(x, recv, c, at, lines, lines + i, lines + col, index(line, a, core))
            for i, a in enumerate(other_cols)
        ]

    def to_cores(x, recv, c):
        at = place(0, 0, core)
        return [
            remote(
                x, recv, c, at, lines * across, lines + across + i,
                lines + across + core, index(line, col, k),
            )
            for i, k in enumerate(other_cores)
        ]

    def send_own(x, recv, c):
        for copy in to_lines(x, recv, c):
            copy.start()

    def pass_on(x, recv, c):
        for l in other_lines:
            remote(x, recv, c, place(l, col, core), 1, 0, l, index(l, col, core)).wait_recv()
        for copy in to_cols(x, recv, c):
            copy.start()

    def finish(x, recv, c):
        for a in other_cols:
            remote(
                x, recv, c, place(0, a, core), lines, 0, lines + a, index(line, a, core)
            ).wait_recv()
        for copy in to_cores(x, recv, c):
            copy.start()

    def settle(x, recv, c):
        for k in other_cores:
            remote(
                x, recv, c, place(0, 0, k), lines * across, 0, lines + across + k,
                index(line, col, k),
            ).wait_recv()

    def drain(x, recv, c):
        for copy in to_lines(x, recv, c) + to_cols(x, recv, c) + to_cores(x, recv, c):
            copy.wait_send()

    def gathered(x, c):
        block = x[c].astype(jnp.float32).reshape(devices * rows, width)
        return block.astype(jnp.bfloat16)

    @pl.loop(0, chunks)
    def _(c):
        send_own(x1, recv1, c)

    middle = HEAD_DIM // 2
    lane = lax.broadcasted_iota(jnp.int32, (rows, HEAD_DIM), 1)
    which = lax.broadcasted_iota(jnp.int32, (rows, HEAD_DIM), 0)
    position = jnp.zeros((rows, HEAD_DIM), jnp.float32)
    for r in range(rows):
        position = jnp.where(which == r, len_ref[r].astype(jnp.float32), position)
    offsets = jnp.where(lane < middle, lane, lane - middle).astype(jnp.float32)
    angles = position * jnp.exp(offsets * (-2.0 * math.log(rope_base) / HEAD_DIM))
    sine = jnp.sin(angles)
    tables[0] = jnp.concatenate([jnp.cos(angles)] * per_group, axis=0)
    tables[1] = jnp.concatenate([jnp.where(lane < middle, -sine, sine)] * per_group, axis=0)

    kv_copy.wait()
    acc[...] = jnp.zeros_like(acc)
    acc_kv[...] = jnp.zeros_like(acc_kv)
    early = min(2, chunks)
    for c in range(early):
        pass_on(x1, recv1, c)
    finish(x1, recv1, 0)

    @pl.loop(0, chunks)
    def _(c):
        @pl.when(c + early < chunks)
        def _():
            pass_on(x1, recv1, c + early)

        @pl.when(c + 1 < chunks)
        def _():
            finish(x1, recv1, c + 1)

        settle(x1, recv1, c)
        weights(wq_ref, c).wait()
        x = gathered(x1, c)
        acc[...] += jnp.dot(x, wbuf[c], preferred_element_type=jnp.float32)
        acc_kv[...] += jnp.dot(
            x,
            kvbuf[pl.ds(pl.multiple_of(c * width, width), width), :],
            preferred_element_type=jnp.float32,
        )
        weights(wo_ref, c).start()

    to_peers[:, :, :q_cols] = acc[...].reshape(devices, rows, q_cols).astype(jnp.bfloat16)
    to_peers[:, :, q_cols:] = acc_kv[...].reshape(devices, rows, kv_cols).astype(jnp.bfloat16)

    def exchange(i):
        target = lax.rem(me + i, devices)
        return pltpu.make_async_remote_copy(
            src_ref=to_peers.at[place_of(target)],
            dst_ref=from_peers.at[me],
            send_sem=peer_send.at[i],
            recv_sem=peer_recv.at[me],
            device_id={"mp": target},
            device_id_type=MESH,
        )

    def exchanged(i):
        source = lax.rem(me + i, devices)
        return pltpu.make_async_remote_copy(
            src_ref=to_peers.at[place_of(source)],
            dst_ref=from_peers.at[source],
            send_sem=peer_send.at[i],
            recv_sem=peer_recv.at[source],
            device_id={"mp": source},
            device_id_type=MESH,
        )

    @pl.loop(1, devices)
    def _(i):
        exchange(i).start()

    from_peers[me] = to_peers[mine]

    @pl.loop(0, chunks)
    def _(c):
        drain(x1, recv1, c)

    k_copy.wait()
    v_copy.wait()

    @pl.loop(1, devices)
    def _(i):
        exchanged(i).wait_recv()

    @pl.loop(1, devices)
    def _(i):
        exchange(i).wait_send()

    scaling = 1.0 / math.sqrt(HEAD_DIM)

    def turn(v, c, s):
        swapped = jnp.concatenate([v[:, middle:], v[:, :middle]], axis=1)
        return (v * c + swapped * s).astype(jnp.bfloat16).astype(jnp.float32)

    def pair_head(j):
        if hkv == 1:
            return from_peers[j, :, q_cols:].astype(jnp.float32)
        at = pl.multiple_of(q_cols + lax.rem(j, hkv) * HEAD_DIM, HEAD_DIM)
        return from_peers[j // hkv, :, pl.ds(at, HEAD_DIM)].astype(jnp.float32)

    passing = min(3, chunks)
    finishing = min(5, chunks)

    @pl.loop(0, groups)
    def _(g):
        @pl.when(g >= passing)
        def _():
            pass_on(x2, recv2, g - passing)

        @pl.when(g >= finishing)
        def _():
            finish(x2, recv2, g - finishing)

        heads = []
        for h in range(per_group):
            owner = g * (per_group // hq) + h // hq
            at = (h % hq) * HEAD_DIM
            heads.append(from_peers[owner, :, at : at + HEAD_DIM].astype(jnp.float32))
        q_rows[...] = turn(jnp.concatenate(heads, axis=0), tables[0], tables[1])
        fresh[0:rows, :] = turn(pair_head(g), tables[0, 0:rows, :], tables[1, 0:rows, :])
        fresh[rows : 2 * rows, :] = pair_head(groups + g)
        slots = kbuf.shape[2]
        slot = lax.broadcasted_iota(jnp.int32, (per_group, slots), 1)
        scores, own = [], []
        for r in range(rows):
            query = q_rows[pl.ds(r, per_group, stride=rows), :]
            own.append(jnp.sum(query * fresh[r : r + 1, :], axis=-1, keepdims=True))
            part = lax.dot_general(
                query.astype(jnp.bfloat16),
                kbuf[r, g],
                (((1,), (1,)), ((), ())),
                preferred_element_type=jnp.float32,
            )
            scores.append(jnp.where(slot < len_ref[r], part * scaling, -1e30))
        scores = jnp.concatenate(scores, axis=0)
        own = jnp.concatenate(own, axis=0) * scaling
        highest = jnp.maximum(jnp.max(scores, axis=-1, keepdims=True), own)
        weight = jnp.exp(scores - highest)
        own_weight = jnp.exp(own - highest)
        scale = 1.0 / (jnp.sum(weight, axis=-1, keepdims=True) + own_weight)
        probs = (weight * scale).astype(jnp.bfloat16)
        own_prob = (own_weight * scale).astype(jnp.bfloat16).astype(jnp.float32)
        mixed = []
        for r in range(rows):
            at = slice(r * per_group, (r + 1) * per_group)
            mixed.append(
                jnp.dot(probs[at], vbuf[r, g], preferred_element_type=jnp.float32)
                + own_prob[at] * fresh[rows + r : rows + r + 1, :]
            )
        for r in range(rows):
            a_rows[pl.ds(r, per_group, stride=rows), :] = mixed[r]
        for h in range(per_group):
            x2[g, mine, :, h * HEAD_DIM : (h + 1) * HEAD_DIM] = a_rows[
                h * rows : (h + 1) * rows, :
            ].astype(jnp.bfloat16)
        send_own(x2, recv2, g)

    acc[...] = jnp.zeros_like(acc)

    @pl.loop(0, chunks)
    def _(c):
        @pl.when(c + chunks - passing < chunks)
        def _():
            pass_on(x2, recv2, c + chunks - passing)

        @pl.when(c + chunks - finishing < chunks)
        def _():
            finish(x2, recv2, c + chunks - finishing)

        settle(x2, recv2, c)
        weights(wo_ref, c).wait()
        acc[...] += jnp.dot(gathered(x2, c), wbuf[c], preferred_element_type=jnp.float32)

    ordered = []
    for l in range(lines):
        for a in range(across):
            for k in range(cores):
                ordered.append(acc[place(l, a, k) * rows : (place(l, a, k) + 1) * rows, :])
    out_ref[...] = jnp.concatenate(ordered, axis=0).astype(jnp.bfloat16)

    @pl.loop(0, chunks)
    def _(c):
        drain(x2, recv2, c)


def fused_shards(
    dims, activations, gain, q_weight, kv_weight, o_weight, key_cache, value_cache, lengths
):
    devices = dims[0] * dims[1] * dims[2]
    rows, features = activations.shape
    q_cols = q_weight.shape[1]
    kv_cols = kv_weight.shape[1]
    chunks = KV_HEADS
    width = features // chunks
    sends = sum(dims)
    vmem = pl.BlockSpec(memory_space=pltpu.VMEM)
    hbm = pl.BlockSpec(memory_space=pl.ANY)
    dma = pltpu.SemaphoreType.DMA
    return pl.pallas_call(
        functools.partial(fused, dims),
        out_shape=jax.ShapeDtypeStruct((devices * rows, o_weight.shape[1]), jnp.bfloat16),
        in_specs=[vmem] * 2 + [pl.BlockSpec(memory_space=pltpu.SMEM)] + [hbm] * 5,
        out_specs=vmem,
        scratch_shapes=[
            pltpu.VMEM((chunks, width, q_cols), jnp.bfloat16),
            pltpu.VMEM(kv_weight.shape, jnp.bfloat16),
            pltpu.VMEM(key_cache.shape, jnp.bfloat16),
            pltpu.VMEM(value_cache.shape, jnp.bfloat16),
            pltpu.VMEM((chunks, devices, rows, width), jnp.bfloat16),
            pltpu.VMEM((chunks, devices, rows, width), jnp.bfloat16),
            pltpu.VMEM((devices * rows, q_cols), jnp.float32),
            pltpu.VMEM((devices * rows, kv_cols), jnp.float32),
            pltpu.VMEM((devices, rows, q_cols + kv_cols), jnp.bfloat16),
            pltpu.VMEM((devices, rows, q_cols + kv_cols), jnp.bfloat16),
            pltpu.VMEM((HEADS // KV_HEADS * rows, HEAD_DIM), jnp.float32),
            pltpu.VMEM((HEADS // KV_HEADS * rows, HEAD_DIM), jnp.float32),
            pltpu.VMEM((2 * rows, HEAD_DIM), jnp.float32),
            pltpu.VMEM((2, HEADS // KV_HEADS * rows, HEAD_DIM), jnp.float32),
            dma((chunks,)),
            dma((1,)),
            dma((2,)),
            dma((chunks, sends)),
            dma((chunks, sends)),
            dma((chunks, sends)),
            dma((devices,)),
            dma((devices,)),
        ],
        compiler_params=pltpu.CompilerParams(
            collective_id=0, has_side_effects=True, vmem_limit_bytes=62 * 1024 * 1024
        ),
    )(
        activations,
        gain,
        lengths,
        q_weight,
        kv_weight,
        o_weight,
        key_cache,
        value_cache,
    )


def fits(mesh):
    devices = mesh.shape["mp"]
    per_group = HEADS // KV_HEADS
    heads = HEADS // devices if HEADS % devices == 0 else 0
    pairs = 2 * KV_HEADS // devices if 2 * KV_HEADS % devices == 0 else 0
    return heads > 0 and pairs > 0 and per_group % heads == 0


def solution(mesh):
    placed = (
        P(("groups", "mp"), None),
        P(),
        P(None, "mp"),
        P(None, "mp"),
        P(None, "mp"),
        P(("groups", "mp"), None, None, None),
        P(("groups", "mp"), None, None, None),
        P(("groups", "mp")),
    )
    body = functools.partial(fused_shards, layout_of(mesh)) if fits(mesh) else shards
    return jax.shard_map(
        body, mesh=mesh, in_specs=placed, out_specs=P("groups", "mp"), check_vma=False
    )
```
